32 devices in a mesh: head: 2 (over y), seq: 16 (over z, x, core).
Axes of the slice: x: 2, y: 2, z: 4, core: 2. Of those that a mesh axis runs over, the one named last changes fastest.
Arguments:
- tokens: bfloat16 [4096, 3072], P(('seq', 'head')), may hold values from -48 to 48
- segment_ids: int32 [4096], replicated, may hold values from 0 to 15, as said below
- lengths: int32 [16], replicated, may hold values from 1 to 1024, as said below
- deal: int32 [16], replicated, may hold values from 0 to 15, each once
- attn_gain: float32 [3072], replicated, may hold values from 0.25 to 1.75
- query_key_value_weight: bfloat16 [3072, 5120], P(None, 'head'), may hold values from -4 to 4
- out_weight: bfloat16 [3072, 3072], P('head'), may hold values from -0.109375 to 0.109375
- mlp_gain: float32 [3072], replicated, may hold values from 0.25 to 1.75
- gate_up_weight: bfloat16 [3072, 2, 4096], P('seq', None, 'head'), may hold values from -0.109375 to 0.109375
- down_weight: bfloat16 [3072, 4096], P('seq', 'head'), may hold values from -0.09375 to 0.09375
Outputs:
- out: bfloat16 [4096, 3072], P(('seq', 'head'))
- key_cache: bfloat16 [8, 4096, 128], P('head', 'seq')
- value_cache: bfloat16 [8, 4096, 128], P('head', 'seq')
The draws below stay inside these ranges and needn't reach their ends.
Inputs may be any that keep to these rules, and one draw needn't show every extreme that they name: lengths[s] is the number of stream tokens of prompt s; they sum to 4096 and the longest is exactly 1024. segment_ids[p] is the prompt holding stream position p; prompts 0 to 15 lie end to end in order with the lengths given by lengths. `deal`: each block number appears once.
All inputs are finite; a program needn't handle non-finite values.
Results may differ from the reference program's by a relative error of at most 0.011.
Values may be sent and summed in bfloat16 or wider, within the bound.
A program may use at most 192 MiB of HBM per device.

```python
import math
import jax
import jax.numpy as jnp
from jax import lax

MODEL_WIDTH = 3072
QUERY_HEAD_COUNT = 24
KEY_VALUE_HEADS = 8
HEAD_WIDTH = 128
FFW = 4096
BLK = 256
PROMPTS = 16
BLOCKS = 16
STREAM_LENGTH = 4096
MOSTLEN = 1024


def prompt_table(key):
    base_rows = (STREAM_LENGTH - MOSTLEN) // (PROMPTS - 1)
    remainder = STREAM_LENGTH - MOSTLEN - base_rows * (PROMPTS - 1)
    spread = base_rows * 3 // 8
    jitter = jax.random.randint(jax.random.fold_in(key, 11), (PROMPTS - 1,), -spread, spread + 1)
    others = base_rows + jitter - jnp.roll(jitter, 1)
    others = others + jnp.where(jnp.arange(PROMPTS - 1) == 0, remainder, 0)
    longest = jax.random.randint(jax.random.fold_in(key, 12), (), 0, PROMPTS)
    prompt_index = jnp.arange(PROMPTS)
    shifted = jnp.clip(prompt_index - (prompt_index > longest).astype(jnp.int32), 0, PROMPTS - 2)
    picked = jnp.take(others, shifted)
    return jnp.where(prompt_index == longest, MOSTLEN, picked).astype(jnp.int32)


def draw_lengths(key, part):
    return prompt_table(key)


def draw_segment_ids(key, part):
    prompt_ends = jnp.cumsum(prompt_table(key)).astype(jnp.int32)
    stream_index = jnp.arange(STREAM_LENGTH, dtype=jnp.int32)
    return jnp.sum((stream_index[None, :] >= prompt_ends[:, None]).astype(jnp.int32), axis=0).astype(jnp.int32)


def draw_tokens(key, part):
    base_rows = jnp.clip(jax.random.normal(jax.random.fold_in(key, 1), (STREAM_LENGTH, MODEL_WIDTH), jnp.float32), -5.0, 5.0)
    row_scale = jnp.exp(jax.random.uniform(jax.random.fold_in(key, 2), (STREAM_LENGTH, 1), jnp.float32, math.log(0.4), math.log(4.0)))
    column_scale = jnp.exp(jax.random.uniform(jax.random.fold_in(key, 3), (1, MODEL_WIDTH), jnp.float32, math.log(0.5), math.log(2.0)))
    return (base_rows * row_scale * column_scale).astype(jnp.bfloat16)


def draw_query_key_value_weight(key, part):
    heads_per_group = QUERY_HEAD_COUNT // KEY_VALUE_HEADS
    scale_of_weight = 1.2 / math.sqrt(MODEL_WIDTH)
    unrotated_part = jnp.clip(jax.random.normal(jax.random.fold_in(key, 20), (MODEL_WIDTH, KEY_VALUE_HEADS, heads_per_group + 2, HEAD_WIDTH), jnp.float32), -6.0, 6.0) * scale_of_weight
    unrotated_part = jnp.clip(unrotated_part, -4.0, 4.0)
    return unrotated_part.reshape(MODEL_WIDTH, KEY_VALUE_HEADS * (heads_per_group + 2) * HEAD_WIDTH).astype(jnp.bfloat16)


def levels(key, shape, pieces, least, high):
    def one(dim, shards_of):
        heights = jax.random.uniform(jax.random.fold_in(jax.random.fold_in(key, 6), dim), (shards_of,), jnp.float32, least / len(pieces), high / len(pieces))
        return jnp.repeat(jnp.exp(heights), shape[dim] // shards_of).reshape((-1,) + (1,) * (len(shape) - dim - 1))

    level = one(*pieces[0])
    for cut in pieces[1:]:
        level = level * one(*cut)
    return level


def gaussian(key, extent, scale, bound, shards=(), kind=jnp.bfloat16):
    array = scale * jax.random.normal(key, extent, jnp.float32)
    if shards:
        array = array * levels(key, extent, shards, -0.22, 0.18)
    return jnp.clip(array, -bound, bound).astype(kind)


def setup_inputs(seed: int = 0) -> dict:
    keys = jax.random.split(jax.random.key(seed), 11)
    tokens = draw_tokens(jax.random.fold_in(keys[10], 71), 0)
    segment_ids = draw_segment_ids(jax.random.fold_in(keys[10], 71), 0)
    lengths = draw_lengths(jax.random.fold_in(keys[10], 71), 0)
    deal = jax.random.permutation(keys[3], BLOCKS).astype(jnp.int32)
    attn_gain = jnp.clip(1.0 + 0.15 * jax.random.normal(keys[4], (MODEL_WIDTH,), jnp.float32), 0.25, 1.75)
    query_key_value_weight = draw_query_key_value_weight(jax.random.fold_in(keys[10], 71), 0)
    out_weight = gaussian(keys[6], (QUERY_HEAD_COUNT * HEAD_WIDTH, MODEL_WIDTH), (QUERY_HEAD_COUNT * HEAD_WIDTH) ** -0.5, 0.109375, ((0, 2),))
    mlp_gain = jnp.clip(1.0 + 0.15 * jax.random.normal(keys[7], (MODEL_WIDTH,), jnp.float32), 0.25, 1.75)
    gate_up_weight = gaussian(keys[8], (MODEL_WIDTH, 2, FFW), MODEL_WIDTH ** -0.5, 0.109375, ((0, 16), (2, 2)))
    down_weight = gaussian(keys[9], (MODEL_WIDTH, FFW), FFW ** -0.5, 0.09375, ((0, 16), (1, 2)))
    return {"tokens": tokens, "segment_ids": segment_ids, "lengths": lengths, "deal": deal, "attn_gain": attn_gain, "query_key_value_weight": query_key_value_weight, "out_weight": out_weight, "mlp_gain": mlp_gain, "gate_up_weight": gate_up_weight, "down_weight": down_weight}


EPSILON = 1e-05
ROPE_BASE = 500000.0

def frequencies(head_size):
    exponent = jnp.arange(0, head_size, 2, dtype=jnp.float32) / head_size
    inverse = 1.0 / ROPE_BASE ** exponent
    wavelength = 2.0 * math.pi / inverse
    smooth = (8192.0 / wavelength - 1.0) / 3.0
    blended = (1.0 - smooth) * inverse / 32.0 + smooth * inverse
    return jnp.where(wavelength > 8192.0, inverse / 32.0, jnp.where(wavelength < 2048.0, inverse, blended))

def rotate(row_values, position, inverse):
    angles = position.astype(jnp.float32)[:, None] * inverse[None, :]
    cosine = jnp.cos(angles)[:, None, None, :]
    sine_term = jnp.sin(angles)[:, None, None, :]
    half_size = row_values.shape[-1] // 2
    first_half = row_values[..., :half_size]
    second_half = row_values[..., half_size:]
    return jnp.concatenate([first_half * cosine - second_half * sine_term, second_half * cosine + first_half * sine_term], axis=-1)

def normalize(row_values, gain_vector):
    values_wide = row_values.astype(jnp.float32)
    factor = lax.rsqrt(lax.optimization_barrier(jnp.mean(values_wide * values_wide, axis=-1, keepdims=True)) + EPSILON)
    return (values_wide * factor * gain_vector.astype(jnp.float32)).astype(jnp.bfloat16)

def reference(tokens, segment_ids, lengths, deal, attn_gain, query_key_value_weight, out_weight, mlp_gain, gate_up_weight, down_weight):
    heads_per_group = QUERY_HEAD_COUNT // KEY_VALUE_HEADS
    row_index = jnp.arange(STREAM_LENGTH, dtype=jnp.int32)
    stream_of_row = (jnp.take(deal, row_index // BLK) * BLK + row_index % BLK).astype(jnp.int32)
    stream_tokens = jnp.zeros_like(tokens).at[stream_of_row].set(tokens)
    starts = (jnp.cumsum(lengths) - lengths).astype(jnp.int32)
    rope_pos = (row_index - jnp.take(starts, segment_ids)).astype(jnp.int32)
    normalized_rows = normalize(stream_tokens, attn_gain)
    projected_rows = jnp.dot(normalized_rows, query_key_value_weight, preferred_element_type=jnp.float32).reshape(STREAM_LENGTH, KEY_VALUE_HEADS, heads_per_group + 2, HEAD_WIDTH)
    inverse = frequencies(HEAD_WIDTH)
    queries = rotate(projected_rows[:, :, :heads_per_group], rope_pos, inverse).astype(jnp.bfloat16)
    key_matrix = rotate(projected_rows[:, :, heads_per_group:heads_per_group + 1], rope_pos, inverse)[:, :, 0].astype(jnp.bfloat16)
    value_matrix = projected_rows[:, :, heads_per_group + 1].astype(jnp.bfloat16)
    qblock = math.gcd(STREAM_LENGTH, 512)
    backward_reach = MOSTLEN
    padded_keys = jnp.concatenate([jnp.zeros((backward_reach, KEY_VALUE_HEADS, HEAD_WIDTH), jnp.bfloat16), key_matrix], axis=0)
    padded_values = jnp.concatenate([jnp.zeros((backward_reach, KEY_VALUE_HEADS, HEAD_WIDTH), jnp.bfloat16), value_matrix], axis=0)
    pad_segments = jnp.concatenate([jnp.full((backward_reach,), -1, jnp.int32), segment_ids.astype(jnp.int32)], axis=0)
    pad_positions = jnp.arange(STREAM_LENGTH + backward_reach, dtype=jnp.int32) - backward_reach
    score_scale = 1.0 / math.sqrt(HEAD_WIDTH)

    def one_block(block_number):
        first_row = (block_number * qblock).astype(jnp.int32)
        window = qblock + backward_reach
        query_block = lax.dynamic_slice_in_dim(queries, first_row, qblock, 0).astype(jnp.float32)
        key_block = lax.dynamic_slice_in_dim(padded_keys, first_row, window, 0).astype(jnp.float32)
        value_block = lax.dynamic_slice_in_dim(padded_values, first_row, window, 0).astype(jnp.float32)
        key_segments = lax.dynamic_slice_in_dim(pad_segments, first_row, window, 0)
        key_positions = lax.dynamic_slice_in_dim(pad_positions, first_row, window, 0)
        query_segments = lax.dynamic_slice_in_dim(segment_ids.astype(jnp.int32), first_row, qblock, 0)
        query_positions = first_row + jnp.arange(qblock, dtype=jnp.int32)
        visible = (query_segments[:, None] == key_segments[None, :]) & (key_positions[None, :] <= query_positions[:, None])
        scores = jnp.einsum('qgjd,kgd->gjqk', query_block, key_block) * score_scale
        masked = jnp.where(visible, scores, -1e+30)
        row_max = lax.optimization_barrier(jnp.max(masked, axis=-1))
        weights = jnp.where(visible, jnp.exp(masked - row_max[..., None]), 0.0)
        row_total = lax.optimization_barrier(jnp.sum(weights, axis=-1))
        rounded = lax.optimization_barrier(weights.astype(jnp.bfloat16)).astype(jnp.float32)
        attention_block = jnp.einsum('gjqk,kgd->qgjd', rounded, value_block)
        attention_block = attention_block / jnp.transpose(row_total, (2, 0, 1))[..., None]
        return attention_block.astype(jnp.bfloat16).reshape(qblock, QUERY_HEAD_COUNT * HEAD_WIDTH)
    attended = lax.map(one_block, jnp.arange(STREAM_LENGTH // qblock, dtype=jnp.int32)).reshape(STREAM_LENGTH, QUERY_HEAD_COUNT * HEAD_WIDTH)
    residual = (stream_tokens.astype(jnp.float32) + jnp.dot(attended, out_weight, preferred_element_type=jnp.float32)).astype(jnp.bfloat16)
    mlp_in = normalize(residual, mlp_gain)
    gate_value = jnp.dot(mlp_in, gate_up_weight[:, 0, :], preferred_element_type=jnp.float32)
    up_value = jnp.dot(mlp_in, gate_up_weight[:, 1, :], preferred_element_type=jnp.float32)
    hidden = (jax.nn.silu(gate_value) * up_value).astype(jnp.bfloat16)
    down_value = jnp.dot(hidden, down_weight.T, preferred_element_type=jnp.float32)
    stream_out = (residual.astype(jnp.float32) + down_value).astype(jnp.bfloat16)
    out = jnp.take(stream_out, stream_of_row, axis=0)
    key_cache = jnp.transpose(jnp.take(key_matrix, stream_of_row, axis=0), (1, 0, 2))
    value_cache = jnp.transpose(jnp.take(value_matrix, stream_of_row, axis=0), (1, 0, 2))
    return (out, key_cache, value_cache)
```

```python
import functools
import math

import jax
import jax.numpy as jnp
from jax import lax
from jax.experimental import pallas as pl
from jax.experimental.pallas import tpu as pltpu
from jax.sharding import PartitionSpec as P

QUERY_HEAD_COUNT = 24
KEY_VALUE_HEADS = 8
HEAD_WIDTH = 128


EPSILON = 1e-05
ROPE_BASE = 500000.0


def frequencies(head_size):
    exponent = jnp.arange(0, head_size, 2, dtype=jnp.float32) / head_size
    inverse = 1.0 / ROPE_BASE**exponent
    wavelength = 2.0 * math.pi / inverse
    smooth = (8192.0 / wavelength - 1.0) / 3.0
    blended = (1.0 - smooth) * inverse / 32.0 + smooth * inverse
    return jnp.where(
        wavelength > 8192.0, inverse / 32.0, jnp.where(wavelength < 2048.0, inverse, blended)
    )


def rotate(row_values, position, inverse):
    angles = position.astype(jnp.float32)[:, None] * inverse[None, :]
    cosine = jnp.cos(angles)[:, None, None, :]
    sine_term = jnp.sin(angles)[:, None, None, :]
    half_size = row_values.shape[-1] // 2
    first_half = row_values[..., :half_size]
    second_half = row_values[..., half_size:]
    return jnp.concatenate(
        [
            first_half * cosine - second_half * sine_term,
            second_half * cosine + first_half * sine_term,
        ],
        axis=-1,
    )


def normalize(row_values, gain_vector):
    values_wide = row_values.astype(jnp.float32)
    factor = lax.rsqrt(jnp.mean(values_wide * values_wide, axis=-1, keepdims=True) + EPSILON)
    return (values_wide * factor * gain_vector).astype(jnp.bfloat16)


def swiglu(gate_up):
    return (jax.nn.silu(gate_up[:, 0]) * gate_up[:, 1]).astype(jnp.bfloat16)


def down_product(hidden, down_rows):
    return lax.dot_general(
        hidden, down_rows, (((1,), (1,)), ((), ())), preferred_element_type=jnp.float32
    )


def shift(values, step, count):
    return lax.ppermute(values, "head", [(i, (i + step) % count) for i in range(count)])


def attention_kernel(window, table_ref, first_ref, start_ref, query_ref, *refs):
    keys = refs[:window]
    values = refs[window : 2 * window]
    out_ref = refs[2 * window]
    block = keys[0].shape[-2]
    query = query_ref[0]
    heads = query.shape[0] // block
    local = jnp.concatenate([start_ref[...]] * heads, axis=0)
    row = lax.broadcasted_iota(jnp.int32, (block, 1), 0)
    row = jnp.concatenate([row] * heads, axis=0)
    key_all = jnp.concatenate([ref[0, 0] for ref in keys], axis=0)
    value_all = jnp.concatenate([ref[0, 0] for ref in values], axis=0)
    scores = lax.dot_general(
        query, key_all, (((1,), (1,)), ((), ())), preferred_element_type=jnp.float32
    ) * (1.0 / math.sqrt(HEAD_WIDTH))
    column = lax.broadcasted_iota(jnp.int32, scores.shape, 1)
    visible = (column >= local) & (column <= row + (window - 1) * block)
    masked = jnp.where(visible, scores, -1e30)
    top = jnp.max(masked, axis=1, keepdims=True)
    weights = jnp.exp(masked - top)
    total = jnp.sum(weights, axis=1, keepdims=True)
    mixed = jnp.dot(weights.astype(jnp.bfloat16), value_all, preferred_element_type=jnp.float32)
    out_ref[0] = (mixed / total).astype(jnp.bfloat16)


def attend(query_heads, pieces, table, local_starts, window):
    groups, rows, width = query_heads.shape
    block = local_starts.shape[0]

    def spec(kind, back):
        return pl.BlockSpec(
            (1, 1, block, width), lambda g, table_ref, first_ref: (kind, g, table_ref[back], 0)
        )

    flops = 4 * groups * rows * window * block * width
    return pl.pallas_call(
        functools.partial(attention_kernel, window),
        grid_spec=pltpu.PrefetchScalarGridSpec(
            num_scalar_prefetch=2,
            grid=(groups,),
            in_specs=[
                pl.BlockSpec((block, 1), lambda g, *_: (0, 0)),
                pl.BlockSpec((1, rows, width), lambda g, *_: (g, 0, 0)),
            ]
            + [spec(0, back) for back in range(window)]
            + [spec(1, back) for back in range(window)],
            out_specs=pl.BlockSpec((1, rows, width), lambda g, *_: (g, 0, 0)),
        ),
        out_shape=jax.ShapeDtypeStruct(query_heads.shape, jnp.bfloat16),
        compiler_params=pltpu.CompilerParams(vmem_limit_bytes=48 * 1024 * 1024),
        cost_estimate=pl.CostEstimate(
            flops=flops,
            bytes_accessed=groups * (rows * 2 + window * block * 2) * width * 2,
            transcendentals=groups * rows * window * block,
        ),
    )(table, table, local_starts, query_heads, *([pieces] * (2 * window)))


def shards(
    tokens,
    segment_ids,
    lengths,
    deal,
    attn_gain,
    query_key_value_weight,
    out_weight,
    mlp_gain,
    gate_up_weight,
    down_weight,
):
    head_count = lax.axis_size("head")
    head_index = lax.axis_index("head")
    seq_index = lax.axis_index("seq")
    rows_here = tokens.shape[0]
    block_rows = rows_here * head_count
    heads_per_group = QUERY_HEAD_COUNT // KEY_VALUE_HEADS
    groups = query_key_value_weight.shape[1] // ((heads_per_group + 2) * HEAD_WIDTH)
    blocks = deal.shape[0]
    longest = segment_ids.shape[0] // 4
    window = min(blocks, -(-(longest - 1) // block_rows) + 1)
    gate_up_all = lax.all_gather(gate_up_weight, "seq", axis=0, tiled=True)
    block_ids = jnp.arange(blocks, dtype=jnp.int32)
    my_block = jnp.sum(jnp.where(block_ids == seq_index, deal, 0))
    stream_pos = my_block * block_rows + jnp.arange(block_rows, dtype=jnp.int32)
    query_segments = lax.dynamic_slice_in_dim(segment_ids, my_block * block_rows, block_rows, 0)
    starts = jnp.cumsum(lengths) - lengths
    prompt_hits = query_segments[:, None] == jnp.arange(lengths.shape[0], dtype=jnp.int32)[None, :]
    query_starts = jnp.sum(jnp.where(prompt_hits, starts[None, :], 0), axis=1)
    rope_pos = stream_pos - query_starts
    wanted = jnp.maximum(my_block - (window - 1) + jnp.arange(window, dtype=jnp.int32), 0)
    table = jnp.sum(
        jnp.where(wanted[:, None] == deal[None, :], block_ids[None, :], 0), axis=1
    ).astype(jnp.int32)
    local_starts = (query_starts - (my_block - (window - 1)) * block_rows)[:, None]
    inverse = frequencies(HEAD_WIDTH)
    full_rows = jnp.zeros((block_rows, tokens.shape[1]), tokens.dtype)
    full_rows = lax.dynamic_update_slice_in_dim(full_rows, tokens, head_index * rows_here, 0)
    for step in range(1, head_count):
        source = (head_index - step) % head_count
        full_rows = lax.dynamic_update_slice_in_dim(
            full_rows, shift(tokens, step, head_count), source * rows_here, 0
        )
    projected_rows = jnp.dot(
        normalize(full_rows, attn_gain), query_key_value_weight, preferred_element_type=jnp.float32
    )
    projected_rows = projected_rows.reshape(block_rows, groups, heads_per_group + 2, HEAD_WIDTH)
    queries = rotate(projected_rows[:, :, :heads_per_group], rope_pos, inverse).astype(jnp.bfloat16)
    key_matrix = rotate(
        projected_rows[:, :, heads_per_group : heads_per_group + 1], rope_pos, inverse
    )[:, :, 0].astype(jnp.bfloat16)
    value_matrix = projected_rows[:, :, heads_per_group + 1].astype(jnp.bfloat16)
    key_cache = jnp.transpose(key_matrix, (1, 0, 2))
    value_cache = jnp.transpose(value_matrix, (1, 0, 2))
    query_heads = jnp.transpose(queries, (1, 2, 0, 3)).reshape(
        groups, heads_per_group * block_rows, HEAD_WIDTH
    )
    key_value = jnp.stack([key_cache, value_cache])
    key_value, gate_up_all = lax.optimization_barrier((key_value, gate_up_all))
    pieces = lax.all_gather(key_value, "seq", axis=2, tiled=True)
    pieces, down_weight = lax.optimization_barrier((pieces, down_weight))
    down_all = lax.all_gather(down_weight, "seq", axis=0, tiled=True)
    attended = attend(query_heads, pieces, table, local_starts, window)
    attended = jnp.transpose(
        attended.reshape(groups, heads_per_group, block_rows, HEAD_WIDTH), (2, 0, 1, 3)
    ).reshape(block_rows, groups * heads_per_group * HEAD_WIDTH)
    part = jnp.dot(attended, out_weight, preferred_element_type=jnp.float32).astype(jnp.bfloat16)
    total_proj = part.astype(jnp.float32)
    for step in range(1, head_count):
        total_proj = total_proj + shift(part, step, head_count).astype(jnp.float32)
    full_residual = (full_rows.astype(jnp.float32) + total_proj).astype(jnp.bfloat16)
    mlp_in = normalize(full_residual, mlp_gain)
    residual = lax.dynamic_slice_in_dim(full_residual, head_index * rows_here, rows_here, 0)
    gate_up = jnp.einsum("rn,nkf->rkf", mlp_in, gate_up_all, preferred_element_type=jnp.float32)
    hidden = swiglu(gate_up)
    down_terms = down_product(hidden, down_all).astype(jnp.bfloat16)
    total = residual.astype(jnp.float32) + lax.dynamic_slice_in_dim(
        down_terms, head_index * rows_here, rows_here, 0
    ).astype(jnp.float32)
    for step in range(1, head_count):
        target = (head_index + step) % head_count
        piece = lax.dynamic_slice_in_dim(down_terms, target * rows_here, rows_here, 0)
        total = total + shift(piece, step, head_count).astype(jnp.float32)
    return (total.astype(jnp.bfloat16), key_cache, value_cache)


def solution(mesh):
    placed = (
        P(("seq", "head"), None),
        P(),
        P(),
        P(),
        P(),
        P(None, "head"),
        P("head", None),
        P(),
        P("seq", None, "head"),
        P("seq", "head"),
    )
    return jax.shard_map(
        shards,
        mesh=mesh,
        in_specs=placed,
        out_specs=(P(("seq", "head"), None), P("head", "seq", None), P("head", "seq", None)),
        check_vma=False,
    )
```

```python
import functools
import math

import jax
import jax.numpy as jnp
from jax import lax
from jax.experimental import pallas as pl
from jax.experimental.pallas import tpu as pltpu
from jax.sharding import PartitionSpec as P

QUERY_HEAD_COUNT = 24
KEY_VALUE_HEADS = 8
HEAD_WIDTH = 128


EPSILON = 1e-05
ROPE_BASE = 500000.0


def frequencies(head_size):
    exponent = jnp.arange(0, head_size, 2, dtype=jnp.float32) / head_size
    inverse = 1.0 / ROPE_BASE**exponent
    wavelength = 2.0 * math.pi / inverse
    smooth = (8192.0 / wavelength - 1.0) / 3.0
    blended = (1.0 - smooth) * inverse / 32.0 + smooth * inverse
    return jnp.where(
        wavelength > 8192.0, inverse / 32.0, jnp.where(wavelength < 2048.0, inverse, blended)
    )


def rotate(row_values, position, inverse):
    angles = position.astype(jnp.float32)[:, None] * inverse[None, :]
    cosine = jnp.cos(angles)[:, None, None, :]
    sine_term = jnp.sin(angles)[:, None, None, :]
    half_size = row_values.shape[-1] // 2
    first_half = row_values[..., :half_size]
    second_half = row_values[..., half_size:]
    return jnp.concatenate(
        [
            first_half * cosine - second_half * sine_term,
            second_half * cosine + first_half * sine_term,
        ],
        axis=-1,
    )


def normalize(row_values, gain_vector):
    values_wide = row_values.astype(jnp.float32)
    factor = lax.rsqrt(jnp.mean(values_wide * values_wide, axis=-1, keepdims=True) + EPSILON)
    return (values_wide * factor * gain_vector).astype(jnp.bfloat16)


def down_product(hidden, down_rows):
    return lax.dot_general(
        hidden, down_rows, (((1,), (1,)), ((), ())), preferred_element_type=jnp.float32
    )


def shift(values, step, count):
    return lax.ppermute(values, "head", [(i, (i + step) % count) for i in range(count)])


def gather_kernel(levels, own_ref, out_ref, copy_sem, up_sem, down_sem, side_sem, core_sem, recv_sem):
    me = lax.axis_index("seq")
    core = me % 2
    side = (me // 2) % 2
    level = me // 4
    has_above = level < levels - 1
    has_below = level > 0

    def slot(at_level, at_side, at_core):
        return at_level * 4 + at_side * 2 + at_core

    up = me + 4
    down = me - 4
    across = me + 2 - 4 * side
    partner = me + 1 - 2 * core

    def copy(source, index, send_sem, target):
        return pltpu.make_async_remote_copy(
            src_ref=source,
            dst_ref=out_ref.at[index],
            send_sem=send_sem,
            recv_sem=recv_sem.at[index],
            device_id={"seq": target},
            device_id_type=pl.DeviceIdType.MESH,
        )

    def arrived(index):
        copy(out_ref.at[index], index, copy_sem, partner).wait_recv()

    def greet(target):
        pl.semaphore_signal(
            barrier, inc=1, device_id={"seq": target}, device_id_type=pl.DeviceIdType.MESH
        )

    barrier = pltpu.get_barrier_semaphore()
    greet(partner)
    greet(across)
    pl.when(has_above)(lambda: greet(up))
    pl.when(has_below)(lambda: greet(down))
    peers = 2 + jnp.where(has_above, 1, 0) + jnp.where(has_below, 1, 0)
    pl.semaphore_wait(barrier, peers)

    pl.when(has_above)(lambda: copy(own_ref, me, up_sem.at[0], up).start())
    pl.when(has_below)(lambda: copy(own_ref, me, down_sem.at[0], down).start())
    copy(own_ref, me, side_sem.at[0], across).start()
    copy(own_ref, me, core_sem.at[0], partner).start()
    keep = pltpu.make_async_copy(own_ref, out_ref.at[me], copy_sem)
    keep.start()

    for far in range(1, levels):

        @pl.when(level - far >= 0)
        def _():
            index = slot(level - far, side, core)
            arrived(index)
            block = out_ref.at[index]
            pl.when(has_above)(lambda: copy(block, index, up_sem.at[far], up).start())
            copy(block, index, side_sem.at[2 * far - 1], across).start()
            copy(block, index, core_sem.at[2 * far - 1], partner).start()

        @pl.when(level + far < levels)
        def _():
            index = slot(level + far, side, core)
            arrived(index)
            block = out_ref.at[index]
            pl.when(has_below)(lambda: copy(block, index, down_sem.at[far], down).start())
            copy(block, index, side_sem.at[2 * far], across).start()
            copy(block, index, core_sem.at[2 * far], partner).start()

    offset = 2 * levels - 1

    def pass_on(at_level, number):
        index = slot(at_level, 1 - side, core)
        arrived(index)
        copy(out_ref.at[index], index, core_sem.at[offset + number], partner).start()

    pass_on(level, 0)
    for far in range(1, levels):
        pl.when(level - far >= 0)(lambda: pass_on(level - far, 2 * far - 1))
        pl.when(level + far < levels)(lambda: pass_on(level + far, 2 * far))

    for at_level in range(levels):
        for at_side in range(2):
            arrived(slot(at_level, at_side, 1 - core))

    keep.wait()

    def sent(sem, target):
        copy(own_ref, me, sem, target).wait_send()

    pl.when(has_above)(lambda: sent(up_sem.at[0], up))
    pl.when(has_below)(lambda: sent(down_sem.at[0], down))
    sent(side_sem.at[0], across)
    sent(core_sem.at[0], partner)
    sent(core_sem.at[offset], partner)
    for far in range(1, levels):

        @pl.when(level - far >= 0)
        def _():
            pl.when(has_above)(lambda: sent(up_sem.at[far], up))
            sent(side_sem.at[2 * far - 1], across)
            sent(core_sem.at[2 * far - 1], partner)
            sent(core_sem.at[offset + 2 * far - 1], partner)

        @pl.when(level + far < levels)
        def _():
            pl.when(has_below)(lambda: sent(down_sem.at[far], down))
            sent(side_sem.at[2 * far], across)
            sent(core_sem.at[2 * far], partner)
            sent(core_sem.at[offset + 2 * far], partner)


def gather_blocks(own, count):
    levels = count // 4
    dma = pltpu.SemaphoreType.DMA
    return pl.pallas_call(
        functools.partial(gather_kernel, levels),
        out_shape=jax.ShapeDtypeStruct((count,) + own.shape, own.dtype),
        in_specs=[pl.BlockSpec(memory_space=pl.ANY)],
        out_specs=pl.BlockSpec(memory_space=pl.ANY),
        scratch_shapes=[
            dma,
            dma((levels,)),
            dma((levels,)),
            dma((2 * levels - 1,)),
            dma((2 * (2 * levels - 1),)),
            dma((count,)),
        ],
        compiler_params=pltpu.CompilerParams(collective_id=0, has_side_effects=True),
        cost_estimate=pl.CostEstimate(flops=0, bytes_accessed=count * own.size * 2, transcendentals=0),
    )(own)


def attention_kernel(window, table_ref, start_ref, query_ref, *refs):
    keys = refs[:window]
    values = refs[window : 2 * window]
    out_ref = refs[2 * window]
    block = keys[0].shape[-2]
    query = query_ref[0]
    heads = query.shape[0] // block
    local = jnp.concatenate([start_ref[...]] * heads, axis=0)
    row = lax.broadcasted_iota(jnp.int32, (block, 1), 0)
    row = jnp.concatenate([row] * heads, axis=0)
    key_all = jnp.concatenate([ref[0, 0, 0] for ref in keys], axis=0)
    value_all = jnp.concatenate([ref[0, 0, 0] for ref in values], axis=0)
    scores = lax.dot_general(
        query, key_all, (((1,), (1,)), ((), ())), preferred_element_type=jnp.float32
    ) * (1.0 / math.sqrt(HEAD_WIDTH))
    column = lax.broadcasted_iota(jnp.int32, scores.shape, 1)
    visible = (column >= local) & (column <= row + (window - 1) * block)
    masked = jnp.where(visible, scores, -1e30)
    top = jnp.max(masked, axis=1, keepdims=True)
    weights = jnp.exp(masked - top)
    total = jnp.sum(weights, axis=1, keepdims=True)
    mixed = jnp.dot(weights.astype(jnp.bfloat16), value_all, preferred_element_type=jnp.float32)
    out_ref[0] = (mixed / total).astype(jnp.bfloat16)


def attend(query_heads, pieces, table, local_starts, window):
    groups, rows, width = query_heads.shape
    block = local_starts.shape[0]

    def spec(kind, back):
        return pl.BlockSpec(
            (1, 1, 1, block, width),
            lambda g, table_ref: (table_ref[back], kind, g, 0, 0),
        )

    flops = 4 * groups * rows * window * block * width
    return pl.pallas_call(
        functools.partial(attention_kernel, window),
        grid_spec=pltpu.PrefetchScalarGridSpec(
            num_scalar_prefetch=1,
            grid=(groups,),
            in_specs=[
                pl.BlockSpec((block, 1), lambda g, *_: (0, 0)),
                pl.BlockSpec((1, rows, width), lambda g, *_: (g, 0, 0)),
            ]
            + [spec(0, back) for back in range(window)]
            + [spec(1, back) for back in range(window)],
            out_specs=pl.BlockSpec((1, rows, width), lambda g, *_: (g, 0, 0)),
        ),
        out_shape=jax.ShapeDtypeStruct(query_heads.shape, jnp.bfloat16),
        compiler_params=pltpu.CompilerParams(vmem_limit_bytes=48 * 1024 * 1024),
        cost_estimate=pl.CostEstimate(
            flops=flops,
            bytes_accessed=groups * (rows * 2 + window * block * 2) * width * 2,
            transcendentals=groups * rows * window * block,
        ),
    )(table, local_starts, query_heads, *([pieces] * (2 * window)))


def shards(
    tokens,
    segment_ids,
    lengths,
    deal,
    attn_gain,
    query_key_value_weight,
    out_weight,
    mlp_gain,
    gate_up_weight,
    down_weight,
):
    head_count = lax.axis_size("head")
    head_index = lax.axis_index("head")
    seq_index = lax.axis_index("seq")
    rows_here = tokens.shape[0]
    block_rows = rows_here * head_count
    heads_per_group = QUERY_HEAD_COUNT // KEY_VALUE_HEADS
    groups = query_key_value_weight.shape[1] // ((heads_per_group + 2) * HEAD_WIDTH)
    blocks = deal.shape[0]
    longest = segment_ids.shape[0] // 4
    window = min(blocks, -(-(longest - 1) // block_rows) + 1)
    hidden_here = gate_up_weight.shape[2]
    weight_rows = jnp.concatenate(
        [gate_up_weight.reshape(gate_up_weight.shape[0], 2 * hidden_here), down_weight], axis=1
    )
    weights_all = lax.all_gather(weight_rows, "seq", axis=0, tiled=True)
    block_ids = jnp.arange(blocks, dtype=jnp.int32)
    my_block = jnp.sum(jnp.where(block_ids == seq_index, deal, 0))
    stream_pos = my_block * block_rows + jnp.arange(block_rows, dtype=jnp.int32)
    query_segments = lax.dynamic_slice_in_dim(segment_ids, my_block * block_rows, block_rows, 0)
    starts = jnp.cumsum(lengths) - lengths
    prompt_hits = query_segments[:, None] == jnp.arange(lengths.shape[0], dtype=jnp.int32)[None, :]
    query_starts = jnp.sum(jnp.where(prompt_hits, starts[None, :], 0), axis=1)
    rope_pos = stream_pos - query_starts
    wanted = jnp.maximum(my_block - (window - 1) + jnp.arange(window, dtype=jnp.int32), 0)
    table = jnp.sum(
        jnp.where(wanted[:, None] == deal[None, :], block_ids[None, :], 0), axis=1
    ).astype(jnp.int32)
    local_starts = (query_starts - (my_block - (window - 1)) * block_rows)[:, None]
    inverse = frequencies(HEAD_WIDTH)
    full_rows = jnp.zeros((block_rows, tokens.shape[1]), tokens.dtype)
    full_rows = lax.dynamic_update_slice_in_dim(full_rows, tokens, head_index * rows_here, 0)
    for step in range(1, head_count):
        source = (head_index - step) % head_count
        full_rows = lax.dynamic_update_slice_in_dim(
            full_rows, shift(tokens, step, head_count), source * rows_here, 0
        )
    projected_rows = jnp.dot(
        normalize(full_rows, attn_gain), query_key_value_weight, preferred_element_type=jnp.float32
    )
    projected_rows = projected_rows.reshape(block_rows, groups, heads_per_group + 2, HEAD_WIDTH)
    queries = rotate(projected_rows[:, :, :heads_per_group], rope_pos, inverse).astype(jnp.bfloat16)
    key_matrix = rotate(
        projected_rows[:, :, heads_per_group : heads_per_group + 1], rope_pos, inverse
    )[:, :, 0].astype(jnp.bfloat16)
    value_matrix = projected_rows[:, :, heads_per_group + 1].astype(jnp.bfloat16)
    key_cache = jnp.transpose(key_matrix, (1, 0, 2))
    value_cache = jnp.transpose(value_matrix, (1, 0, 2))
    query_heads = jnp.transpose(queries, (1, 2, 0, 3)).reshape(
        groups, heads_per_group * block_rows, HEAD_WIDTH
    )
    key_value = jnp.stack([key_cache, value_cache])
    pieces = gather_blocks(key_value, blocks)
    attended = attend(query_heads, pieces, table, local_starts, window)
    attended = jnp.transpose(
        attended.reshape(groups, heads_per_group, block_rows, HEAD_WIDTH), (2, 0, 1, 3)
    ).reshape(block_rows, groups * heads_per_group * HEAD_WIDTH)
    part = jnp.dot(attended, out_weight, preferred_element_type=jnp.float32).astype(jnp.bfloat16)
    total_proj = part.astype(jnp.float32)
    for step in range(1, head_count):
        total_proj = total_proj + shift(part, step, head_count).astype(jnp.float32)
    full_residual = (full_rows.astype(jnp.float32) + total_proj).astype(jnp.bfloat16)
    mlp_in = normalize(full_residual, mlp_gain)
    residual = lax.dynamic_slice_in_dim(full_residual, head_index * rows_here, rows_here, 0)
    gate = jnp.dot(mlp_in, weights_all[:, :hidden_here], preferred_element_type=jnp.float32)
    up = jnp.dot(
        mlp_in, weights_all[:, hidden_here : 2 * hidden_here], preferred_element_type=jnp.float32
    )
    hidden = (jax.nn.silu(gate) * up).astype(jnp.bfloat16)
    down_terms = down_product(hidden, weights_all[:, 2 * hidden_here :]).astype(jnp.bfloat16)
    total = residual.astype(jnp.float32) + lax.dynamic_slice_in_dim(
        down_terms, head_index * rows_here, rows_here, 0
    ).astype(jnp.float32)
    for step in range(1, head_count):
        target = (head_index + step) % head_count
        piece = lax.dynamic_slice_in_dim(down_terms, target * rows_here, rows_here, 0)
        total = total + shift(piece, step, head_count).astype(jnp.float32)
    return (total.astype(jnp.bfloat16), key_cache, value_cache)


def solution(mesh):
    placed = (
        P(("seq", "head"), None),
        P(),
        P(),
        P(),
        P(),
        P(None, "head"),
        P("head", None),
        P(),
        P("seq", None, "head"),
        P("seq", "head"),
    )
    return jax.shard_map(
        shards,
        mesh=mesh,
        in_specs=placed,
        out_specs=(P(("seq", "head"), None), P("head", "seq", None), P("head", "seq", None)),
        check_vma=False,
    )
```

```python
import functools
import math

import jax
import jax.numpy as jnp
from jax import lax
from jax.experimental import pallas as pl
from jax.experimental.pallas import tpu as pltpu
from jax.sharding import PartitionSpec as P

QUERY_HEAD_COUNT = 24
KEY_VALUE_HEADS = 8
HEAD_WIDTH = 128


EPSILON = 1e-05
ROPE_BASE = 500000.0


def frequencies(head_size):
    exponent = jnp.arange(0, head_size, 2, dtype=jnp.float32) / head_size
    inverse = 1.0 / ROPE_BASE**exponent
    wavelength = 2.0 * math.pi / inverse
    smooth = (8192.0 / wavelength - 1.0) / 3.0
    blended = (1.0 - smooth) * inverse / 32.0 + smooth * inverse
    return jnp.where(
        wavelength > 8192.0, inverse / 32.0, jnp.where(wavelength < 2048.0, inverse, blended)
    )


def rotate(row_values, position, inverse):
    angles = position.astype(jnp.float32)[:, None] * inverse[None, :]
    cosine = jnp.cos(angles)[:, None, None, :]
    sine_term = jnp.sin(angles)[:, None, None, :]
    half_size = row_values.shape[-1] // 2
    first_half = row_values[..., :half_size]
    second_half = row_values[..., half_size:]
    return jnp.concatenate(
        [
            first_half * cosine - second_half * sine_term,
            second_half * cosine + first_half * sine_term,
        ],
        axis=-1,
    )


def normalize(row_values, gain_vector):
    values_wide = row_values.astype(jnp.float32)
    factor = lax.rsqrt(jnp.mean(values_wide * values_wide, axis=-1, keepdims=True) + EPSILON)
    return (values_wide * factor * gain_vector).astype(jnp.bfloat16)


def down_product(hidden, down_rows):
    return lax.dot_general(
        hidden, down_rows, (((1,), (1,)), ((), ())), preferred_element_type=jnp.float32
    )


def shift(values, step, count):
    return lax.ppermute(values, "head", [(i, (i + step) % count) for i in range(count)])


def gather_kernel(levels, own_ref, out_ref, copy_sem, up_sem, down_sem, side_sem, core_sem, recv_sem):
    me = lax.axis_index("seq")
    core = me % 2
    side = (me // 2) % 2
    level = me // 4
    has_above = level < levels - 1
    has_below = level > 0

    def slot(at_level, at_side, at_core):
        return at_level * 4 + at_side * 2 + at_core

    up = me + 4
    down = me - 4
    across = me + 2 - 4 * side
    partner = me + 1 - 2 * core

    def copy(source, index, send_sem, target):
        return pltpu.make_async_remote_copy(
            src_ref=source,
            dst_ref=out_ref.at[index],
            send_sem=send_sem,
            recv_sem=recv_sem.at[index],
            device_id={"seq": target},
            device_id_type=pl.DeviceIdType.MESH,
        )

    def arrived(index):
        copy(out_ref.at[index], index, copy_sem, partner).wait_recv()

    def greet(target):
        pl.semaphore_signal(
            barrier, inc=1, device_id={"seq": target}, device_id_type=pl.DeviceIdType.MESH
        )

    barrier = pltpu.get_barrier_semaphore()
    greet(partner)
    greet(across)
    pl.when(has_above)(lambda: greet(up))
    pl.when(has_below)(lambda: greet(down))
    peers = 2 + jnp.where(has_above, 1, 0) + jnp.where(has_below, 1, 0)
    pl.semaphore_wait(barrier, peers)

    pl.when(has_above)(lambda: copy(own_ref, me, up_sem.at[0], up).start())
    pl.when(has_below)(lambda: copy(own_ref, me, down_sem.at[0], down).start())
    copy(own_ref, me, side_sem.at[0], across).start()
    copy(own_ref, me, core_sem.at[0], partner).start()
    keep = pltpu.make_async_copy(own_ref, out_ref.at[me], copy_sem)
    keep.start()

    for far in range(1, levels):

        @pl.when(level - far >= 0)
        def _():
            index = slot(level - far, side, core)
            arrived(index)
            block = out_ref.at[index]
            pl.when(has_above)(lambda: copy(block, index, up_sem.at[far], up).start())
            copy(block, index, side_sem.at[2 * far - 1], across).start()
            copy(block, index, core_sem.at[2 * far - 1], partner).start()

        @pl.when(level + far < levels)
        def _():
            index = slot(level + far, side, core)
            arrived(index)
            block = out_ref.at[index]
            pl.when(has_below)(lambda: copy(block, index, down_sem.at[far], down).start())
            copy(block, index, side_sem.at[2 * far], across).start()
            copy(block, index, core_sem.at[2 * far], partner).start()

    offset = 2 * levels - 1

    def pass_on(at_level, number):
        index = slot(at_level, 1 - side, core)
        arrived(index)
        copy(out_ref.at[index], index, core_sem.at[offset + number], partner).start()

    pass_on(level, 0)
    for far in range(1, levels):
        pl.when(level - far >= 0)(lambda: pass_on(level - far, 2 * far - 1))
        pl.when(level + far < levels)(lambda: pass_on(level + far, 2 * far))

    for at_level in range(levels):
        for at_side in range(2):
            arrived(slot(at_level, at_side, 1 - core))

    keep.wait()

    def sent(sem, target):
        copy(own_ref, me, sem, target).wait_send()

    pl.when(has_above)(lambda: sent(up_sem.at[0], up))
    pl.when(has_below)(lambda: sent(down_sem.at[0], down))
    sent(side_sem.at[0], across)
    sent(core_sem.at[0], partner)
    sent(core_sem.at[offset], partner)
    for far in range(1, levels):

        @pl.when(level - far >= 0)
        def _():
            pl.when(has_above)(lambda: sent(up_sem.at[far], up))
            sent(side_sem.at[2 * far - 1], across)
            sent(core_sem.at[2 * far - 1], partner)
            sent(core_sem.at[offset + 2 * far - 1], partner)

        @pl.when(level + far < levels)
        def _():
            pl.when(has_below)(lambda: sent(down_sem.at[far], down))
            sent(side_sem.at[2 * far], across)
            sent(core_sem.at[2 * far], partner)
            sent(core_sem.at[offset + 2 * far], partner)


def gather_blocks(own, count):
    levels = count // 4
    dma = pltpu.SemaphoreType.DMA
    return pl.pallas_call(
        functools.partial(gather_kernel, levels),
        out_shape=jax.ShapeDtypeStruct((count,) + own.shape, own.dtype),
        in_specs=[pl.BlockSpec(memory_space=pl.ANY)],
        out_specs=pl.BlockSpec(memory_space=pl.ANY),
        scratch_shapes=[
            dma,
            dma((levels,)),
            dma((levels,)),
            dma((2 * levels - 1,)),
            dma((2 * (2 * levels - 1),)),
            dma((count,)),
        ],
        compiler_params=pltpu.CompilerParams(collective_id=0, has_side_effects=True),
        cost_estimate=pl.CostEstimate(flops=0, bytes_accessed=count * own.size * 2, transcendentals=0),
    )(own)


def attention_kernel(window, table_ref, start_ref, query_ref, *refs):
    keys = refs[:window]
    values = refs[window : 2 * window]
    out_ref = refs[2 * window]
    block = keys[0].shape[-2]
    query = query_ref[0]
    heads = query.shape[0] // block
    local = jnp.concatenate([start_ref[...]] * heads, axis=0)
    row = lax.broadcasted_iota(jnp.int32, (block, 1), 0)
    row = jnp.concatenate([row] * heads, axis=0)
    key_all = jnp.concatenate([ref[0, 0, 0] for ref in keys], axis=0)
    value_all = jnp.concatenate([ref[0, 0, 0] for ref in values], axis=0)
    scores = lax.dot_general(
        query, key_all, (((1,), (1,)), ((), ())), preferred_element_type=jnp.float32
    ) * (1.0 / math.sqrt(HEAD_WIDTH))
    column = lax.broadcasted_iota(jnp.int32, scores.shape, 1)
    visible = (column >= local) & (column <= row + (window - 1) * block)
    masked = jnp.where(visible, scores, -1e30)
    top = jnp.max(masked, axis=1, keepdims=True)
    weights = jnp.exp(masked - top)
    total = jnp.sum(weights, axis=1, keepdims=True)
    mixed = jnp.dot(weights.astype(jnp.bfloat16), value_all, preferred_element_type=jnp.float32)
    out_ref[0] = (mixed / total).astype(jnp.bfloat16)


def attend(query_heads, pieces, table, local_starts, window):
    groups, rows, width = query_heads.shape
    block = local_starts.shape[0]

    def spec(kind, back):
        return pl.BlockSpec(
            (1, 1, 1, block, width),
            lambda g, table_ref: (table_ref[back], kind, g, 0, 0),
        )

    flops = 4 * groups * rows * window * block * width
    return pl.pallas_call(
        functools.partial(attention_kernel, window),
        grid_spec=pltpu.PrefetchScalarGridSpec(
            num_scalar_prefetch=1,
            grid=(groups,),
            in_specs=[
                pl.BlockSpec((block, 1), lambda g, *_: (0, 0)),
                pl.BlockSpec((1, rows, width), lambda g, *_: (g, 0, 0)),
            ]
            + [spec(0, back) for back in range(window)]
            + [spec(1, back) for back in range(window)],
            out_specs=pl.BlockSpec((1, rows, width), lambda g, *_: (g, 0, 0)),
        ),
        out_shape=jax.ShapeDtypeStruct(query_heads.shape, jnp.bfloat16),
        compiler_params=pltpu.CompilerParams(vmem_limit_bytes=48 * 1024 * 1024),
        cost_estimate=pl.CostEstimate(
            flops=flops,
            bytes_accessed=groups * (rows * 2 + window * block * 2) * width * 2,
            transcendentals=groups * rows * window * block,
        ),
    )(table, local_starts, query_heads, *([pieces] * (2 * window)))


def shards(
    tokens,
    segment_ids,
    lengths,
    deal,
    attn_gain,
    query_key_value_weight,
    out_weight,
    mlp_gain,
    gate_up_weight,
    down_weight,
):
    head_count = lax.axis_size("head")
    head_index = lax.axis_index("head")
    seq_index = lax.axis_index("seq")
    rows_here = tokens.shape[0]
    block_rows = rows_here * head_count
    heads_per_group = QUERY_HEAD_COUNT // KEY_VALUE_HEADS
    groups = query_key_value_weight.shape[1] // ((heads_per_group + 2) * HEAD_WIDTH)
    blocks = deal.shape[0]
    longest = segment_ids.shape[0] // 4
    window = min(blocks, -(-(longest - 1) // block_rows) + 1)
    hidden_here = gate_up_weight.shape[2]
    weight_rows = jnp.concatenate(
        [gate_up_weight.reshape(gate_up_weight.shape[0], 2 * hidden_here), down_weight], axis=1
    )
    weights_all = lax.all_gather(weight_rows, "seq", axis=0, tiled=True)
    block_ids = jnp.arange(blocks, dtype=jnp.int32)
    my_block = jnp.sum(jnp.where(block_ids == seq_index, deal, 0))
    stream_pos = my_block * block_rows + jnp.arange(block_rows, dtype=jnp.int32)
    query_segments = lax.dynamic_slice_in_dim(segment_ids, my_block * block_rows, block_rows, 0)
    starts = jnp.cumsum(lengths) - lengths
    prompt_hits = query_segments[:, None] == jnp.arange(lengths.shape[0], dtype=jnp.int32)[None, :]
    query_starts = jnp.sum(jnp.where(prompt_hits, starts[None, :], 0), axis=1)
    rope_pos = stream_pos - query_starts
    wanted = jnp.maximum(my_block - (window - 1) + jnp.arange(window, dtype=jnp.int32), 0)
    table = jnp.sum(
        jnp.where(wanted[:, None] == deal[None, :], block_ids[None, :], 0), axis=1
    ).astype(jnp.int32)
    local_starts = (query_starts - (my_block - (window - 1)) * block_rows)[:, None]
    inverse = frequencies(HEAD_WIDTH)
    full_rows = jnp.zeros((block_rows, tokens.shape[1]), tokens.dtype)
    full_rows = lax.dynamic_update_slice_in_dim(full_rows, tokens, head_index * rows_here, 0)
    for step in range(1, head_count):
        source = (head_index - step) % head_count
        full_rows = lax.dynamic_update_slice_in_dim(
            full_rows, shift(tokens, step, head_count), source * rows_here, 0
        )
    projected_rows = jnp.dot(
        normalize(full_rows, attn_gain), query_key_value_weight, preferred_element_type=jnp.float32
    )
    projected_rows = projected_rows.reshape(block_rows, groups, heads_per_group + 2, HEAD_WIDTH)
    queries = rotate(projected_rows[:, :, :heads_per_group], rope_pos, inverse).astype(jnp.bfloat16)
    key_matrix = rotate(
        projected_rows[:, :, heads_per_group : heads_per_group + 1], rope_pos, inverse
    )[:, :, 0].astype(jnp.bfloat16)
    value_matrix = projected_rows[:, :, heads_per_group + 1].astype(jnp.bfloat16)
    key_cache = jnp.transpose(key_matrix, (1, 0, 2))
    value_cache = jnp.transpose(value_matrix, (1, 0, 2))
    query_heads = jnp.transpose(queries, (1, 2, 0, 3)).reshape(
        groups, heads_per_group * block_rows, HEAD_WIDTH
    )
    key_value = jnp.stack([key_cache, value_cache])
    pieces = gather_blocks(key_value, blocks)
    attended = attend(query_heads, pieces, table, local_starts, window)
    attended = jnp.transpose(
        attended.reshape(groups, heads_per_group, block_rows, HEAD_WIDTH), (2, 0, 1, 3)
    ).reshape(block_rows, groups * heads_per_group * HEAD_WIDTH)
    part = jnp.dot(attended, out_weight, preferred_element_type=jnp.float32).astype(jnp.bfloat16)
    total_proj = part.astype(jnp.float32)
    for step in range(1, head_count):
        total_proj = total_proj + shift(part, step, head_count).astype(jnp.float32)
    full_residual = (full_rows.astype(jnp.float32) + total_proj).astype(jnp.bfloat16)
    mlp_in = lax.optimization_barrier(normalize(full_residual, mlp_gain))
    residual = lax.dynamic_slice_in_dim(full_residual, head_index * rows_here, rows_here, 0)
    gate = jnp.dot(mlp_in, weights_all[:, :hidden_here], preferred_element_type=jnp.float32)
    up = jnp.dot(
        mlp_in, weights_all[:, hidden_here : 2 * hidden_here], preferred_element_type=jnp.float32
    )
    hidden = (jax.nn.silu(gate) * up).astype(jnp.bfloat16)
    chunks = []
    pieces_down = 3
    width = weights_all.shape[0] // pieces_down
    for number in range(pieces_down):
        columns = slice(number * width, (number + 1) * width)
        terms = down_product(hidden, weights_all[columns, 2 * hidden_here :]).astype(jnp.bfloat16)
        total = residual[:, columns].astype(jnp.float32) + lax.dynamic_slice_in_dim(
            terms, head_index * rows_here, rows_here, 0
        ).astype(jnp.float32)
        for step in range(1, head_count):
            target = (head_index + step) % head_count
            piece = lax.dynamic_slice_in_dim(terms, target * rows_here, rows_here, 0)
            total = total + shift(piece, step, head_count).astype(jnp.float32)
        chunks.append(total.astype(jnp.bfloat16))
    output = jnp.concatenate(chunks, axis=1)
    return (output, key_cache, value_cache)


def solution(mesh):
    placed = (
        P(("seq", "head"), None),
        P(),
        P(),
        P(),
        P(),
        P(None, "head"),
        P("head", None),
        P(),
        P("seq", None, "head"),
        P("seq", "head"),
    )
    return jax.shard_map(
        shards,
        mesh=mesh,
        in_specs=placed,
        out_specs=(P(("seq", "head"), None), P("head", "seq", None), P("head", "seq", None)),
        check_vma=False,
    )
```
